32 devices in a mesh: batch: 4 (over z), seq: 8 (over y, x, core).
Axes of the slice: x: 2, y: 2, z: 4, core: 2. Of those that a mesh axis runs over, the one named last changes fastest.
Arguments:
- resid_in: bfloat16 [8, 512, 2048], P('batch', 'seq'), may hold values from -6 to 6
- cotangent: bfloat16 [8, 512, 2048], P('batch', 'seq'), may hold values from -6 to 6
- segments: int32 [8, 512], P('batch'), may hold values from 0 to 2, never falling along the last dimension, each value on 1 to 256 neighbouring positions
- norm_gain: float32 [2048], P(('batch', 'seq')), may hold values from 0.5 to 1.5
- in_proj: float32 [2048, 8192], P(('batch', 'seq')), may hold values from -0.125 to 0.125
- conv_weight: float32 [4, 4096], P(None, ('batch', 'seq')), may hold values from -0.5 to 0.5
- conv_bias: float32 [4096], P(('batch', 'seq')), may hold values from -0.5 to 0.5
- x_proj: float32 [4096, 160], P(('batch', 'seq')), may hold values from -0.09375 to 0.09375
- dt_proj: float32 [128, 4096], P(None, ('batch', 'seq')), may hold values from -0.5 to 0.5
- dt_bias: float32 [4096], P(('batch', 'seq')), may hold values from -4.6 to -1
- a_log: float32 [16, 4096], P(None, ('batch', 'seq')), may hold values from -1.5 to 2.8
- skip_gain: float32 [4096], P(('batch', 'seq')), may hold values from 0.5 to 1.5
- out_proj: float32 [4096, 2048], P(('batch', 'seq')), may hold values from -0.375 to 0.375
Outputs:
- resid_out: bfloat16 [8, 512, 2048], P('batch', 'seq')
- grad_in: bfloat16 [8, 512, 2048], P('batch', 'seq')
- grad_norm_gain: float32 [2048], P(('batch', 'seq'))
- grad_in_proj: float32 [2048, 8192], P(('batch', 'seq'))
- grad_conv_weight: float32 [4, 4096], P(None, ('batch', 'seq'))
- grad_conv_bias: float32 [4096], P(('batch', 'seq'))
- grad_x_proj: float32 [4096, 160], P(('batch', 'seq'))
- grad_dt_proj: float32 [128, 4096], P(None, ('batch', 'seq'))
- grad_dt_bias: float32 [4096], P(('batch', 'seq'))
- grad_a_log: float32 [16, 4096], P(None, ('batch', 'seq'))
- grad_skip_gain: float32 [4096], P(('batch', 'seq'))
- grad_out_proj: float32 [4096, 2048], P(('batch', 'seq'))
The draws below stay inside these ranges and needn't reach their ends.
Inputs may be any that keep to these rules, and one draw needn't show every extreme that they name: `segments`: in each sequence the numbers start at 0, never fall and rise by one where a document begins; every number up to the largest is used; no document is longer than min(2000, 256) positions and some document has exactly that many.
All inputs are finite; a program needn't handle non-finite values.
Results may differ from the reference program's by a relative error of at most 0.012.
The reference program's roundings to bfloat16 on the way count: a program that leaves them out, or rounds other values in their place, can miss the bound.
Values may be sent and summed in bfloat16 or wider, within the bound.
No kernel may reach another device: no remote copies, remote signals or barrier semaphores. Data moves between devices by JAX's collectives and lax.ppermute only.
A program may use at most 320 MiB of HBM per device.

```python
import math
import jax
import jax.numpy as jnp
import numpy as np
from jax import lax

MODEL = 2048
INNER = 4096
STATE = 16
RANK = 128
KERNEL = 4
BLOCK = 16
SEQS = 8
LENGTH = 512


def level_of(own_key, shape, shards, low, high):
    level = 1.0
    for axis_at, blocks in shards:
        heights = jax.random.uniform(jax.random.fold_in(jax.random.fold_in(own_key, 6), axis_at), (blocks,), jnp.float32, low / len(shards), high / len(shards))
        level = level * jnp.repeat(jnp.exp(heights), shape[axis_at] // blocks).reshape((-1,) + (1,) * (len(shape) - 1 - axis_at))
    return level


def split_up(number_of, total, most, skew):
    loads = [(1 << 20) // math.isqrt(grade ** skew) + 1 for grade in range(2, number_of + 1)]
    spare, counts = total - most - (number_of - 1), [1] * (number_of - 1)
    while spare > 0:
        free = [i for i in range(number_of - 1) if counts[i] < most]
        mass, budget = sum([loads[i] for i in free]), spare
        for i in free:
            addition = min(most - counts[i], max(1, budget * loads[i] // mass), spare)
            counts[i] = counts[i] + addition
            spare = spare - addition
    return np.array([most] + counts)


def uneven(stream_key, count, total, most, skew):
    if count == 2:
        one = jax.random.randint(stream_key, (), max(1, total - most), min(most, total - 1) + 1)
        return jnp.stack([one, total - one])
    lengths = jnp.asarray(split_up(count, total, most, skew), jnp.int32)
    couples = (count - 1) // 2
    donor, sink = lengths[1:1 + 2 * couples:2], lengths[2:2 + 2 * couples:2]
    room = jnp.minimum(donor - 1, most - sink)
    passed = jax.random.randint(jax.random.fold_in(stream_key, 1), (couples,), 0, 1 << 20) % (room + 1)
    lengths = lengths.at[1:1 + 2 * couples:2].set(donor - passed).at[2:2 + 2 * couples:2].set(sink + passed)
    return lengths[jax.random.permutation(jax.random.fold_in(stream_key, 2), count)]


def bell_draw(rng, dims, spread, bound, cuts=(), dtype=jnp.bfloat16):
    entries = spread * jax.random.normal(rng, dims, jnp.float32)
    if cuts:
        entries = entries * level_of(rng, dims, cuts, -0.22, 0.18)
    return jnp.clip(entries, -bound, bound).astype(dtype)


def setup_inputs(seed: int = 0) -> dict:
    streams_of = jax.random.split(jax.random.key(seed), 14)
    resid_in = bell_draw(streams_of[0], (SEQS, LENGTH, MODEL), 1.0, 6.0, ((0, 4), (1, 8)))
    cotangent = bell_draw(streams_of[1], (SEQS, LENGTH, MODEL), 1.0, 6.0, ((0, 4), (1, 8)))
    segments = jax.vmap(lambda own: jnp.searchsorted(jnp.cumsum(uneven(own, LENGTH // 600 + 3, LENGTH, min(2000, LENGTH // 2), 0)), jnp.arange(LENGTH), side="right"))(jax.random.split(streams_of[2], SEQS)).reshape((SEQS, LENGTH)).astype(jnp.int32)
    norm_gain = jnp.clip(1.0 + 0.1 * jax.random.normal(streams_of[3], (MODEL,), jnp.float32), 0.5, 1.5)
    in_proj = bell_draw(streams_of[4], (MODEL, 2 * INNER), MODEL ** -0.5, 0.125, ((0, 32),), jnp.float32)
    conv_weight = jnp.clip(jax.random.uniform(streams_of[5], (KERNEL, INNER), jnp.float32, -0.5, 0.5) * level_of(streams_of[5], (KERNEL, INNER), ((1, 32),), -0.4, 0.0), -0.5, 0.5)
    conv_bias = jnp.clip(jax.random.uniform(streams_of[6], (INNER,), jnp.float32, -0.5, 0.5) * level_of(streams_of[6], (INNER,), ((0, 32),), -0.4, 0.0), -0.5, 0.5)
    x_proj = bell_draw(streams_of[7], (INNER, RANK + 2 * STATE), INNER ** -0.5, 0.09375, ((0, 32),), jnp.float32)
    dt_proj = bell_draw(streams_of[8], (RANK, INNER), RANK ** -0.5, 0.5, ((1, 32),), jnp.float32)
    dt_bias = jnp.clip(-4.6 + 3.6 * jax.random.uniform(streams_of[9], (INNER,), jnp.float32) ** level_of(streams_of[9], (INNER,), ((0, 32),), -0.2, 0.2), -4.6, -1.0)
    a_log = jnp.clip(-1.5 + 4.3 * jax.random.uniform(streams_of[10], (STATE, INNER), jnp.float32) ** level_of(streams_of[10], (STATE, INNER), ((1, 32),), -0.2, 0.2), -1.5, 2.8)
    skip_gain = jnp.clip(0.5 + 1.0 * jax.random.uniform(streams_of[11], (INNER,), jnp.float32) ** level_of(streams_of[11], (INNER,), ((0, 32),), -0.2, 0.2), 0.5, 1.5)
    out_proj = bell_draw(streams_of[12], (INNER, MODEL), (INNER // 16) ** -0.5, 0.375, ((0, 32),), jnp.float32)
    return {"resid_in": resid_in, "cotangent": cotangent, "segments": segments, "norm_gain": norm_gain, "in_proj": in_proj, "conv_weight": conv_weight, "conv_bias": conv_bias, "x_proj": x_proj, "dt_proj": dt_proj, "dt_bias": dt_bias, "a_log": a_log, "skip_gain": skip_gain, "out_proj": out_proj}


EPSILON = 1e-05

@jax.custom_vjp
def low(v):
    return lax.optimization_barrier(v.astype(jnp.bfloat16)).astype(jnp.float32)

@jax.custom_vjp
def low_back(v):
    return v

def low_keep(v):
    return (low(v), None)

def low_pass(kept, grad):
    return (grad,)

def back_keep(v):
    return (v, None)

def back_low(kept, grad):
    return (low(grad),)
low.defvjp(low_keep, low_pass)
low_back.defvjp(back_keep, back_low)

def product(left, right):
    return jnp.dot(left, right, precision=lax.Precision.HIGHEST, preferred_element_type=jnp.float32)

def selective(step_size, activated, inject, readout, same_doc, decay_rate):
    length = step_size.shape[0]
    blocks = length // BLOCK

    def advance(current, pieces):
        step_now, act_now, inject_now, readout_now, same_now = pieces
        decay_now = jnp.exp(step_now[None, :] * decay_rate) * same_now
        current = decay_now * current + inject_now[:, None] * (step_now * act_now)[None, :]
        return (current, lax.optimization_barrier(jnp.sum(current * readout_now[:, None], axis=0)))

    def run_block(current, pieces):
        return lax.scan(advance, current, pieces)
    pieces = tuple((v.reshape((blocks, BLOCK) + v.shape[1:]) for v in (step_size, activated, inject, readout, same_doc)))
    _, scanned = lax.scan(jax.checkpoint(run_block), jnp.zeros((STATE, INNER), jnp.float32), pieces)
    return scanned.reshape(length, INNER)

def mamba_layer(residual, seg_ids, norm_gain, in_proj, conv_weight, conv_bias, x_proj, dt_proj, dt_bias, a_log, skip_gain, out_proj):
    length = residual.shape[0]
    rms_scale = lax.rsqrt(lax.optimization_barrier(jnp.mean(residual * residual, axis=-1, keepdims=True)) + EPSILON)
    normed = low(residual * rms_scale * low(norm_gain))
    mixed_in = low_back(product(normed, low(in_proj)))
    signal = low(mixed_in[:, :INNER])
    gate_pre = mixed_in[:, INNER:]
    padded = jnp.concatenate([jnp.zeros((KERNEL - 1, INNER), jnp.float32), signal], axis=0)
    seg_pad = jnp.concatenate([jnp.full((KERNEL - 1,), -1, jnp.int32), seg_ids.astype(jnp.int32)], axis=0)
    conv_taps = low(conv_weight)
    pre_conv = low(conv_bias)
    for k in range(KERNEL):
        allowed = (seg_pad[k:k + length] == seg_ids).astype(jnp.float32)
        pre_conv = pre_conv + conv_taps[k] * padded[k:k + length] * allowed[:, None]
    same_doc = (seg_pad[KERNEL - 2:KERNEL - 2 + length] == seg_ids).astype(jnp.float32)
    activated = low(jax.nn.silu(pre_conv))
    projected = low_back(product(activated, low(x_proj)))
    step_low = low(projected[:, :RANK])
    inject = projected[:, RANK:RANK + STATE]
    readout = projected[:, RANK + STATE:]
    step_pre = low_back(product(step_low, low(dt_proj)) + low(dt_bias))
    step_size = jax.nn.softplus(step_pre)
    decay_rate = -jnp.exp(low(a_log))
    scanned = selective(step_size, activated, inject, readout, same_doc, decay_rate)
    mixer = scanned + low(skip_gain) * activated
    gated_out = low(mixer * jax.nn.silu(gate_pre))
    return residual + product(gated_out, low(out_proj))

def reference(resid_in, cotangent, segments, norm_gain, in_proj, conv_weight, conv_bias, x_proj, dt_proj, dt_bias, a_log, skip_gain, out_proj):
    masters = (norm_gain.astype(jnp.float32), in_proj.astype(jnp.float32), conv_weight.astype(jnp.float32), conv_bias.astype(jnp.float32), x_proj.astype(jnp.float32), dt_proj.astype(jnp.float32), dt_bias.astype(jnp.float32), a_log.astype(jnp.float32), skip_gain.astype(jnp.float32), out_proj.astype(jnp.float32))

    def accumulate(running, pieces):
        residual, upstream, seg_ids = pieces

        def forward(resid_value, *weights):
            return mamba_layer(resid_value, seg_ids, *weights)
        result, pull = jax.vjp(forward, residual.astype(jnp.float32), *masters)
        grads = pull(upstream.astype(jnp.float32))
        running = tuple((a + b for a, b in zip(running, grads[1:])))
        return (running, (result.astype(jnp.bfloat16), grads[0].astype(jnp.bfloat16)))
    zeros = tuple((jnp.zeros_like(w) for w in masters))
    totals, (outputs, grad_inputs) = lax.scan(accumulate, zeros, (resid_in, cotangent, segments))
    return (outputs, grad_inputs, totals[0], totals[1], totals[2], totals[3], totals[4], totals[5], totals[6], totals[7], totals[8], totals[9])
```

```python
import jax
import jax.numpy as jnp
from jax import lax
from jax.experimental import pallas as pl
from jax.experimental.pallas import tpu as pltpu
from jax.sharding import Mesh
from jax.sharding import PartitionSpec as P

INNER = 4096
STATE = 16
RANK = 128
KERNEL = 4
SHARD_LEN = 64
BLOCK = 16


EPSILON = 1e-05


def passed_along(value, axis, steps):
    count = lax.axis_size(axis)
    first, last = (max(0, -steps), min(count, count - steps))
    return lax.ppermute(value, axis, [(source, source + steps) for source in range(first, last)])


def prefix(shard, axis, combine, identity, reverse):
    devices, here = (lax.axis_size(axis), lax.axis_index(axis))
    everything = jax.tree.map(lambda part: lax.all_gather(part, axis), shard)
    start = jax.tree.map(
        lambda part, zero: jnp.broadcast_to(jnp.asarray(zero, part.dtype), part.shape),
        shard,
        identity,
    )

    def step(k, before):
        at = devices - 1 - k if reverse else k
        reached = at > here if reverse else at < here
        new = combine(before, jax.tree.map(lambda part: part[at], everything))
        return jax.tree.map(lambda a, b: jnp.where(reached, a, b), new, before)

    return lax.fori_loop(0, devices, step, start)


def for_sending(shard):

    def short(part):
        return part.astype(jnp.bfloat16) if part.dtype == jnp.float32 else part

    return jax.tree.map(short, shard)


def silu_slope(values):
    logistic = jax.nn.sigmoid(values)
    return logistic * (1.0 + values * (1.0 - logistic))


def combine_states(earlier, latter):
    return (earlier[0] * latter[0], latter[0] * earlier[1] + latter[1])


def blocked(values):
    return values.reshape((values.shape[0] // BLOCK, BLOCK) + values.shape[1:])


def decay_of(step_now, same_now, decay_rate):
    return jnp.exp(step_now[:, None, :] * decay_rate) * same_now[:, None, None]


def reduce_blocks(spacing, keeper, column_side, state_side, decay_rate):

    def add_block(running, pieces):
        spacing_b, keeper_b, column_b, state_b = pieces
        weight = jnp.exp(spacing_b[:, :, None, :] * decay_rate) * keeper_b[:, :, None, None]
        return (
            running + jnp.sum(weight * column_b[:, :, None, :] * state_b[:, :, :, None], axis=0),
            None,
        )

    initial = jnp.zeros((column_side.shape[1],) + decay_rate.shape, jnp.float32)
    running, _ = lax.scan(
        add_block,
        initial,
        (blocked(spacing), blocked(keeper), blocked(column_side), blocked(state_side)),
    )
    return running


def forward_states(incoming, step_size, drive_in, inject, readout, same_doc, decay_rate):

    def forward_advance(current, pieces):
        step_now, drive_now, inject_now, readout_now, same_now = pieces
        current = (
            decay_of(step_now, same_now, decay_rate) * current
            + inject_now[:, :, None] * drive_now[:, None, :]
        )
        return (current, jnp.sum(current * readout_now[:, :, None], axis=1))

    def forward_run_block(current, pieces):
        last_state, outputs = lax.scan(forward_advance, current, pieces)
        return (last_state, (current, outputs))

    pieces = (
        blocked(step_size),
        blocked(drive_in),
        blocked(inject),
        blocked(readout),
        blocked(same_doc),
    )
    _, (starts, scanned) = lax.scan(forward_run_block, incoming, pieces)
    return (starts, scanned.reshape(step_size.shape))


def backward_states(
    outgoing, starts, step_size, drive_in, inject, readout, same_doc, grad_mixer, decay_rate
):

    def backward_advance(current, pieces):
        step_now, drive_now, inject_now, same_now = pieces
        current = (
            decay_of(step_now, same_now, decay_rate) * current
            + inject_now[:, :, None] * drive_now[:, None, :]
        )
        return (current, current)

    def retreat(carried, pieces):
        behind, rate_sum = carried
        state_now, previous, step_now, drive_now, inject_now, readout_now, same_now, grad_now = (
            pieces
        )
        decay_now = decay_of(step_now, same_now, decay_rate)
        grad_state = behind + readout_now[:, :, None] * grad_now[:, None, :]
        through = grad_state * previous * decay_now
        outputs = (
            jnp.sum(grad_now[:, None, :] * state_now, axis=-1),
            jnp.sum(grad_state * drive_now[:, None, :], axis=-1),
            jnp.sum(grad_state * inject_now[:, :, None], axis=1),
            jnp.sum(through * decay_rate, axis=1),
        )
        rate_sum = rate_sum + jnp.sum(through * step_now[:, None, :], axis=0)
        return ((decay_now * grad_state, rate_sum), outputs)

    def backward_run_block(carried, pieces):
        begin_state, step_b, drive_b, inject_b, readout_b, same_b, grad_b = pieces
        _, states = lax.scan(backward_advance, begin_state, (step_b, drive_b, inject_b, same_b))
        previous = jnp.concatenate([begin_state[None], states[:-1]], axis=0)
        return lax.scan(
            retreat,
            carried,
            (states, previous, step_b, drive_b, inject_b, readout_b, same_b, grad_b),
            reverse=True,
        )

    pieces = (
        starts,
        blocked(step_size),
        blocked(drive_in),
        blocked(inject),
        blocked(readout),
        blocked(same_doc),
        blocked(grad_mixer),
    )
    (_, rate_sum), outputs = lax.scan(
        backward_run_block,
        (outgoing, jnp.zeros(decay_rate.shape, jnp.float32)),
        pieces,
        reverse=True,
    )
    length = step_size.shape[0]
    return (rate_sum, tuple((v.reshape((length,) + v.shape[2:]) for v in outputs)))


def on_device(
    resid_in,
    cotangent,
    segments,
    norm_gain,
    in_proj,
    conv_weight,
    conv_bias,
    x_proj,
    dt_proj,
    dt_bias,
    a_log,
    skip_gain,
    out_proj,
):
    fetched = (
        lax.all_gather(norm_gain.astype(jnp.bfloat16), ("batch", "seq"), axis=0, tiled=True),
        lax.all_gather(in_proj.astype(jnp.bfloat16), ("batch", "seq"), axis=0, tiled=True),
        lax.all_gather(conv_weight.astype(jnp.bfloat16), ("batch", "seq"), axis=1, tiled=True),
        lax.all_gather(conv_bias.astype(jnp.bfloat16), ("batch", "seq"), axis=0, tiled=True),
        lax.all_gather(x_proj.astype(jnp.bfloat16), ("batch", "seq"), axis=0, tiled=True),
        lax.all_gather(dt_proj.astype(jnp.bfloat16), ("batch", "seq"), axis=1, tiled=True),
        lax.all_gather(dt_bias.astype(jnp.bfloat16), ("batch", "seq"), axis=0, tiled=True),
        lax.all_gather(a_log.astype(jnp.bfloat16), ("batch", "seq"), axis=1, tiled=True),
        lax.all_gather(skip_gain.astype(jnp.bfloat16), ("batch", "seq"), axis=0, tiled=True),
        lax.all_gather(out_proj.astype(jnp.bfloat16), ("batch", "seq"), axis=0, tiled=True),
    )
    (
        gain_low,
        proj_in,
        taps_low,
        shift_low,
        proj_x,
        proj_step,
        bias_low,
        alog_low,
        skip_low,
        proj_out,
    ) = fetched
    norm_scale = gain_low.astype(jnp.float32)
    conv_taps = taps_low.astype(jnp.float32)
    conv_shift = shift_low.astype(jnp.float32)
    step_bias = bias_low.astype(jnp.float32)
    decay_rate = -jnp.exp(alog_low.astype(jnp.float32))
    skip_scale = skip_low.astype(jnp.float32)
    residual = resid_in.astype(jnp.float32)
    rms_scale = lax.rsqrt(jnp.mean(residual * residual, axis=-1, keepdims=True) + EPSILON)
    normed = (residual * rms_scale * norm_scale).astype(jnp.bfloat16)
    mixed_in = jnp.einsum("gtm,mk->tgk", normed, proj_in, preferred_element_type=jnp.float32)
    signal = mixed_in[:, :, :INNER].astype(jnp.bfloat16)
    gate_pre = mixed_in[:, :, INNER:]
    earlier_rows = passed_along(signal[SHARD_LEN - KERNEL + 1 :], "seq", 1)
    extended = jnp.concatenate([earlier_rows, signal], axis=0).astype(jnp.float32)
    offset = lax.axis_index("seq") * SHARD_LEN
    padded_seg = jnp.concatenate(
        [jnp.full((segments.shape[0], KERNEL), -1, jnp.int32), segments], axis=1
    )
    seg_window = lax.dynamic_slice_in_dim(padded_seg, offset + 1, SHARD_LEN + KERNEL - 1, axis=1).T
    seg_own = seg_window[KERNEL - 1 :]
    allowed = [
        (seg_window[k : k + SHARD_LEN] == seg_own).astype(jnp.float32)[:, :, None]
        for k in range(KERNEL)
    ]
    same_doc = allowed[KERNEL - 2][:, :, 0]
    pre_conv = conv_shift + sum(
        (conv_taps[k] * extended[k : k + SHARD_LEN] * allowed[k] for k in range(KERNEL))
    )
    activated = jax.nn.silu(pre_conv).astype(jnp.bfloat16)
    act_value = activated.astype(jnp.float32)
    projected = jnp.einsum("tgi,ik->tgk", activated, proj_x, preferred_element_type=jnp.float32)
    step_low = projected[:, :, :RANK].astype(jnp.bfloat16)
    inject = projected[:, :, RANK : RANK + STATE]
    readout = projected[:, :, RANK + STATE :]
    step_pre = (
        jnp.einsum("tgr,ri->tgi", step_low, proj_step, preferred_element_type=jnp.float32)
        + step_bias
    )
    step_size = jax.nn.softplus(step_pre)
    drive_in = step_size * act_value
    elapsed = jnp.cumsum(step_size, axis=0)
    before_mask = jnp.cumprod(same_doc, axis=0)
    after_mask = jnp.concatenate(
        [jnp.cumprod(same_doc[::-1], axis=0)[::-1][1:], jnp.ones_like(same_doc[:1])], axis=0
    )
    through_all = jnp.exp(elapsed[-1][:, None, :] * decay_rate) * before_mask[-1][:, None, None]
    local_end = reduce_blocks(elapsed[-1] - elapsed, after_mask, drive_in, inject, decay_rate)
    _, incoming = prefix(
        (through_all, local_end),
        "seq",
        combine_states,
        (jnp.ones_like(local_end), jnp.zeros_like(local_end)),
        False,
    )
    starts, scanned = forward_states(
        incoming, step_size, drive_in, inject, readout, same_doc, decay_rate
    )
    mixer = scanned + skip_scale * act_value
    gate_act = jax.nn.silu(gate_pre)
    gated_out = (mixer * gate_act).astype(jnp.bfloat16)
    resid_out = (
        residual
        + jnp.einsum("tgi,im->gtm", gated_out, proj_out, preferred_element_type=jnp.float32)
    ).astype(jnp.bfloat16)
    proj_in, proj_x, proj_step, proj_out = (
        lax.all_gather(in_proj.astype(jnp.bfloat16), ("batch", "seq"), axis=0, tiled=True),
        lax.all_gather(x_proj.astype(jnp.bfloat16), ("batch", "seq"), axis=0, tiled=True),
        lax.all_gather(dt_proj.astype(jnp.bfloat16), ("batch", "seq"), axis=1, tiled=True),
        lax.all_gather(out_proj.astype(jnp.bfloat16), ("batch", "seq"), axis=0, tiled=True),
    )
    upstream = cotangent.astype(jnp.float32)
    grad_out_proj = jnp.einsum(
        "tgi,gtm->im", gated_out, cotangent, preferred_element_type=jnp.float32
    )
    grad_gated = jnp.einsum("gtm,im->tgi", cotangent, proj_out, preferred_element_type=jnp.float32)
    grad_mixer = grad_gated * gate_act
    grad_gate_pre = grad_gated * mixer * silu_slope(gate_pre)
    grad_skip = jnp.sum(grad_mixer * act_value, axis=(0, 1))
    local_start = reduce_blocks(elapsed, before_mask, grad_mixer, readout, decay_rate)
    _, outgoing = prefix(
        (through_all, local_start),
        "seq",
        combine_states,
        (jnp.ones_like(local_start), jnp.zeros_like(local_start)),
        True,
    )
    rate_sum, (grad_readout, grad_inject, grad_drive, grad_step_decay) = backward_states(
        outgoing, starts, step_size, drive_in, inject, readout, same_doc, grad_mixer, decay_rate
    )
    grad_step = grad_step_decay + grad_drive * act_value
    grad_step_pre = (grad_step * jax.nn.sigmoid(step_pre)).astype(jnp.bfloat16)
    grad_dt_bias = jnp.sum(grad_step_pre.astype(jnp.float32), axis=(0, 1))
    grad_dt_proj = jnp.einsum(
        "tgr,tgi->ri", step_low, grad_step_pre, preferred_element_type=jnp.float32
    )
    grad_step_low = jnp.einsum(
        "tgi,ri->tgr", grad_step_pre, proj_step, preferred_element_type=jnp.float32
    )
    grad_projected = jnp.concatenate([grad_step_low, grad_inject, grad_readout], axis=-1).astype(
        jnp.bfloat16
    )
    grad_x_proj = jnp.einsum(
        "tgi,tgk->ik", activated, grad_projected, preferred_element_type=jnp.float32
    )
    grad_act = (
        grad_drive * step_size
        + grad_mixer * skip_scale
        + jnp.einsum("tgk,ik->tgi", grad_projected, proj_x, preferred_element_type=jnp.float32)
    )
    grad_a_log = rate_sum * decay_rate
    grad_pre = grad_act * silu_slope(pre_conv)
    grad_conv_bias = jnp.sum(grad_pre, axis=(0, 1))
    masked = [grad_pre * allowed[k] for k in range(KERNEL)]
    grad_conv_weight = jnp.stack(
        [jnp.sum(extended[k : k + SHARD_LEN] * masked[k], axis=(0, 1)) for k in range(KERNEL)],
        axis=0,
    )
    grad_extended = sum(
        (
            jnp.pad(conv_taps[k] * masked[k], ((k, KERNEL - 1 - k), (0, 0), (0, 0)))
            for k in range(KERNEL)
        )
    )
    returned = passed_along(for_sending(grad_extended[: KERNEL - 1]), "seq", -1)
    grad_signal = grad_extended[KERNEL - 1 :] + jnp.pad(
        returned, ((SHARD_LEN - KERNEL + 1, 0), (0, 0), (0, 0))
    )
    grad_mixed = jnp.concatenate([grad_signal, grad_gate_pre], axis=-1).astype(jnp.bfloat16)
    grad_in_proj = jnp.einsum("gtm,tgk->mk", normed, grad_mixed, preferred_element_type=jnp.float32)
    grad_normed = jnp.einsum("tgk,mk->gtm", grad_mixed, proj_in, preferred_element_type=jnp.float32)
    weighted = grad_normed * norm_scale
    grad_norm_gain = jnp.sum(grad_normed * residual * rms_scale, axis=(0, 1))
    grad_in = (
        upstream
        + rms_scale * weighted
        - residual * rms_scale**3 * jnp.mean(residual * weighted, axis=-1, keepdims=True)
    ).astype(jnp.bfloat16)
    shares = (
        lax.psum_scatter(grad_norm_gain, ("batch", "seq"), scatter_dimension=0, tiled=True),
        lax.psum_scatter(grad_in_proj, ("batch", "seq"), scatter_dimension=0, tiled=True),
        lax.psum_scatter(grad_conv_weight, ("batch", "seq"), scatter_dimension=1, tiled=True),
        lax.psum_scatter(grad_conv_bias, ("batch", "seq"), scatter_dimension=0, tiled=True),
        lax.psum_scatter(grad_x_proj, ("batch", "seq"), scatter_dimension=0, tiled=True),
        lax.psum_scatter(grad_dt_proj, ("batch", "seq"), scatter_dimension=1, tiled=True),
        lax.psum_scatter(grad_dt_bias, ("batch", "seq"), scatter_dimension=0, tiled=True),
        lax.psum_scatter(grad_a_log, ("batch", "seq"), scatter_dimension=1, tiled=True),
        lax.psum_scatter(grad_skip, ("batch", "seq"), scatter_dimension=0, tiled=True),
        lax.psum_scatter(grad_out_proj, ("batch", "seq"), scatter_dimension=0, tiled=True),
    )
    return (
        resid_out,
        grad_in,
        shares[0],
        shares[1],
        shares[2],
        shares[3],
        shares[4],
        shares[5],
        shares[6],
        shares[7],
        shares[8],
        shares[9],
    )


AXES = ("zh", "zl", "y", "x", "c")
GROUP = AXES[1:]
LOG2E = 1.4426950408889634
LN2 = 0.6931471805599453
FAR = 1e30


def swap(value, axis):
    return lax.ppermute(value, axis, [(0, 1), (1, 0)])


def wide(value):
    return value.astype(jnp.float32)


def short(value):
    return value.astype(jnp.bfloat16)


def softplus(v):
    return jnp.maximum(v, 0.0) + jnp.log1p(jnp.exp(-jnp.abs(v)))


def silu(v):
    return v * jax.nn.sigmoid(v)


def pre_activation(before, block, mask, taps, shift, ext):
    ext[8:72, :] = block
    ext[0:8, :] = before
    total = shift + taps[3:4, :] * block
    for k in range(3):
        total = total + taps[k : k + 1, :] * ext[5 + k : 69 + k, :] * mask[:, k : k + 1]
    return total


def conv_kernel(own, sig, masks, taps, shift, xp, act, part, tail, ext):
    own_z, own_p, own_c = own[0], own[1], own[2]
    tail[...] = jnp.zeros_like(tail)

    def step(p, carry):
        rows = []
        for q in range(4):
            zl, i = q // 2, q % 2
            block = wide(sig[(p & 1) ^ own_c, zl ^ own_z, (p >> 1) ^ own_p, i])
            mask = masks[q, pl.ds(pl.multiple_of(p * 64, 64), 64), :]
            pre = pre_activation(tail[q], block, mask, taps, shift[...], ext)
            tail[q] = block[56:64, :]
            low = short(silu(pre))
            act[zl, p, i] = low
            rows.append(low)
        out = jnp.dot(
            jnp.concatenate(rows, axis=0), xp[...], preferred_element_type=jnp.float32
        )
        for q in range(4):
            part[q // 2, p, q % 2] = short(out[q * 64 : q * 64 + 64])
        return carry

    lax.fori_loop(0, 8, step, 0)


def spread(ref, q, g, values):
    ref[pl.ds(q * 2 + g, 64, stride=8), :] = values


def gathered(ref, q, g):
    return ref[pl.ds(q * 2 + g, 64, stride=8), :]


def lane(vector, n):
    return jnp.broadcast_to(vector[:, n : n + 1], (8, 128))


def forward_kernel(
    own, proj, act, gate, masks, dt, dt_bias, rate, skip, states, gated, mixer, st, dr, bc, ys, hs
):
    own_z = own[0]

    @pl.when(pl.program_id(0) == 0)
    def _():
        hs[...] = jnp.zeros_like(hs)

    for q in range(4):
        zl, i = q // 2, q % 2
        pr = proj[zl, 0, i]
        step = softplus(
            jnp.dot(pr[:, :128], dt[...], preferred_element_type=jnp.float32) + dt_bias[...]
        )
        both = wide(pr[:, 128:192])
        small = both[:, :32] + both[:, 32:64]
        far = jnp.where(masks[q][:, 2:3] > 0.0, step, FAR)
        drive = step * wide(act[zl, 0, i])
        for g in range(2):
            spread(st, q, g, far[:, g * 128 : g * 128 + 128])
            spread(dr, q, g, drive[:, g * 128 : g * 128 + 128])
            spread(bc, q, g, small)

    def advance(t, h):
        at = pl.ds(pl.multiple_of(t * 8, 8), 8)
        s, d, b = st[at, :], dr[at, :], bc[at, :]
        y = jnp.zeros((8, 128), jnp.float32)
        new = []
        for n in range(16):
            v = jnp.exp2(s * rate[n]) * h[n] + lane(b, n) * d
            y = y + lane(b, 16 + n) * v
            states[t, n] = v
            new.append(v)
        ys[at, :] = y
        return tuple(new)

    last = lax.fori_loop(0, 64, advance, tuple(hs[n] for n in range(16)), unroll=2)
    for n in range(16):
        hs[n] = last[n]
    for q in range(4):
        zl, i = q // 2, q % 2
        dz = zl ^ own_z
        for g in range(2):
            cols = slice(g * 128, g * 128 + 128)
            m = gathered(ys, q, g) + skip[:, cols] * wide(act[zl, 0, i, :, cols])
            mixer[0, dz, 0, i, :, cols] = m
            gated[0, dz, 0, i, :, cols] = short(m * silu(gate[0, dz, 0, i, :, cols]))


def backward_kernel(
    own, proj, act, dmix, masks, states, prior, dt, dt_bias, rate, skip, pick,
    dproj, dact, g_rate, g_dt, g_bias, g_skip,
    st, sp, dr, dm, bc, dd, ds, pp, rs, gs, low_all, dsp_all,
):
    own_z = own[0]

    @pl.when(pl.program_id(0) == 0)
    def _():
        gs[...] = jnp.zeros_like(gs)
        g_rate[...] = jnp.zeros_like(g_rate)
        g_dt[...] = jnp.zeros_like(g_dt)
        g_bias[...] = jnp.zeros_like(g_bias)
        g_skip[...] = jnp.zeros_like(g_skip)

    slopes, steps = [], []
    for q in range(4):
        zl, i = q // 2, q % 2
        pr = proj[zl, 0, i]
        low_all[q * 64 : q * 64 + 64, :] = pr[:, :128]
        pre = jnp.dot(pr[:, :128], dt[...], preferred_element_type=jnp.float32) + dt_bias[...]
        step = softplus(pre)
        both = wide(pr[:, 128:192])
        small = both[:, :32] + both[:, 32:64]
        far = jnp.where(masks[q][:, 2:3] > 0.0, step, FAR)
        a = wide(act[zl, 0, i])
        drive = step * a
        m = dmix[0, zl ^ own_z, 0, i]
        g_skip[...] += jnp.sum(m * a, axis=0, keepdims=True)
        for g in range(2):
            cols = slice(g * 128, g * 128 + 128)
            spread(st, q, g, far[:, cols])
            spread(sp, q, g, step[:, cols])
            spread(dr, q, g, drive[:, cols])
            spread(dm, q, g, m[:, cols])
            spread(bc, q, g, small)

    def retreat(t, before, carry):
        g, total = carry
        at = pl.ds(pl.multiple_of(t * 8, 8), 8)
        s, step, d, m, b = st[at, :], sp[at, :], dr[at, :], dm[at, :], bc[at, :]
        drive = jnp.zeros((8, 128), jnp.float32)
        change = jnp.zeros((8, 128), jnp.float32)
        new, sums, inj, read = [], [], [], []
        for n in range(16):
            gn = g[n] + lane(b, 16 + n) * m
            read.append(states[t, n] * m)
            inj.append(gn * d)
            drive = drive + gn * lane(b, n)
            back = gn * jnp.exp2(s * rate[n])
            through = back * before(n)
            change = change + through * rate[n]
            sums.append(total[n] + through * step)
            new.append(back)
        dd[at, :] = drive
        ds[at, :] = change
        return (tuple(new), tuple(sums)), inj, read

    def pair(k, carry, first):
        t = 62 - 2 * k
        carry, inj1, read1 = retreat(t + 1, lambda n: states[t, n], carry)
        if first:
            carry, inj0, read0 = retreat(t, lambda n: prior[0, n], carry)
        else:
            carry, inj0, read0 = retreat(t, lambda n: states[t - 1, n], carry)
        at = pl.ds(pl.multiple_of(t * 8, 16), 16)
        for n in range(16):
            cols = slice(n * 128, n * 128 + 128)
            pp[at, cols] = short(jnp.concatenate([inj0[n], inj1[n]], axis=0))
            cols = slice(2048 + n * 128, 2048 + n * 128 + 128)
            pp[at, cols] = short(jnp.concatenate([read0[n], read1[n]], axis=0))
        return carry

    carry = (tuple(gs[n] for n in range(16)), tuple(g_rate[n] for n in range(16)))
    carry = lax.fori_loop(0, 31, lambda k, c: pair(k, c, False), carry)
    g, total = pair(31, carry, True)
    for n in range(16):
        gs[n] = g[n]
        g_rate[n] = total[n]
    rs[...] = jnp.dot(pp[...], pick[...], preferred_element_type=jnp.float32)
    for q in range(4):
        zl, i = q // 2, q % 2
        pr = proj[zl, 0, i]
        pre = jnp.dot(pr[:, :128], dt[...], preferred_element_type=jnp.float32) + dt_bias[...]
        slope = jax.nn.sigmoid(pre)
        for g in range(2):
            cols = slice(g * 128, g * 128 + 128)
            a = wide(act[zl, 0, i, :, cols])
            drive = gathered(dd, q, g)
            dstep = gathered(ds, q, g) * LN2 + drive * a
            dsp = short(dstep * slope[:, cols])
            dsp_all[q * 64 : q * 64 + 64, cols] = dsp
            dact[zl, 0, i, :, cols] = (
                drive * gathered(sp, q, g) + gathered(dm, q, g) * skip[:, cols]
            )
    g_bias[...] += jnp.sum(wide(dsp_all[...]), axis=0, keepdims=True)
    g_dt[...] += lax.dot_general(
        low_all[...], dsp_all[...], (((0,), (0,)), ((), ())), preferred_element_type=jnp.float32
    )
    dlow = lax.dot_general(
        dsp_all[...], dt[...], (((1,), (1,)), ((), ())), preferred_element_type=jnp.float32
    )
    for q in range(4):
        zl, i = q // 2, q % 2
        dproj[zl, 0, i, :, 0:128] = short(dlow[q * 64 : q * 64 + 64])
        small = gathered(rs, q, 0) + gathered(rs, q, 1)
        dproj[zl, 0, i, :, 128:160] = short(small[:, :32])


def conv_back_kernel(
    own, sig, act, dact, dproj, masks, taps, shift, xp, dsig, g_xp, g_taps, g_shift, ext, halo, rows
):
    own_z, own_p, own_c = own[0], own[1], own[2]
    halo[...] = jnp.zeros_like(halo)
    g_xp[...] = jnp.zeros_like(g_xp)
    g_taps[...] = jnp.zeros_like(g_taps)
    g_shift[...] = jnp.zeros_like(g_shift)

    def step(k, carry):
        p = 7 - k
        e = jnp.maximum(p - 1, 0)
        dps = jnp.concatenate([dproj[q // 2, p, q % 2] for q in range(4)], axis=0)
        acts = jnp.concatenate([act[q // 2, p, q % 2] for q in range(4)], axis=0)
        g_xp[...] += lax.dot_general(
            acts, dps, (((0,), (0,)), ((), ())), preferred_element_type=jnp.float32
        )
        more = lax.dot_general(
            dps, xp[...], (((1,), (1,)), ((), ())), preferred_element_type=jnp.float32
        )
        for q in range(4):
            zl, i = q // 2, q % 2
            block = wide(sig[(p & 1) ^ own_c, zl ^ own_z, (p >> 1) ^ own_p, i])
            earlier = wide(sig[(e & 1) ^ own_c, zl ^ own_z, (e >> 1) ^ own_p, i])
            mask = masks[q, pl.ds(pl.multiple_of(p * 64, 64), 64), :]
            pre = pre_activation(earlier[56:64, :], block, mask, taps, shift[...], ext)
            logistic = jax.nn.sigmoid(pre)
            slope = logistic * (1.0 + pre * (1.0 - logistic))
            dpre = (dact[zl, p, i] + more[q * 64 : q * 64 + 64]) * slope
            g_shift[...] += jnp.sum(dpre, axis=0, keepdims=True)
            g_taps[3:4, :] += jnp.sum(dpre * block, axis=0, keepdims=True)
            total = taps[3:4, :] * dpre
            for j in range(3):
                masked = dpre * mask[:, j : j + 1]
                g_taps[j : j + 1, :] += jnp.sum(
                    masked * ext[5 + j : 69 + j, :], axis=0, keepdims=True
                )
                rows[0:64, :] = masked
                rows[64:72, :] = halo[q, j]
                halo[q, j] = masked[0:8, :]
                total = total + taps[j : j + 1, :] * rows[3 - j : 67 - j, :]
            dsig[(p & 1) ^ own_c, zl ^ own_z, (p >> 1) ^ own_p, i] = short(total)
        return carry

    lax.fori_loop(0, 8, step, 0)


def whole(shape):
    return pl.BlockSpec(shape, lambda *_: (0,) * len(shape))


def gather_fast(shard):
    got = {(0, 0, 0): shard}
    for key, axis in (((0, 0, 1), "x"), ((0, 1, 0), "y"), ((1, 0, 0), "zl")):
        got[key] = swap(shard, axis)
    got[0, 1, 1] = swap(got[0, 1, 0], "x")
    got[1, 1, 0] = swap(got[1, 0, 0], "y")
    got[1, 0, 1] = swap(got[0, 0, 1], "zl")
    pieces = (
        swap(got[1, 1, 0][..., :768], "x"),
        swap(got[1, 0, 1][..., 768:1408], "y"),
        swap(got[0, 1, 1][..., 1408:], "zl"),
    )
    got[1, 1, 1] = jnp.concatenate(pieces, axis=-1)
    order = [(a, b, c) for a in range(2) for b in range(2) for c in range(2)]
    mine = [got[key] for key in order]
    return mine + [swap(v, "c") for v in mine]


def gather_slow(shard):
    value = shard[None]
    for axis in ("x", "y", "zl", "c"):
        value = jnp.concatenate([value, swap(value, axis)], axis=0)
    return value


def scatter_slow(keep, recv_from):
    value = wide(keep) + wide(recv_from)
    for axis in ("zl", "y", "x"):
        half = value.shape[0] // 2
        value = value[:half] + wide(swap(short(value[half:]), axis))
    return value[0]


def scatter_fast(value):
    (q0, qx, qy, qyx, qz, qzx, qzy, q3) = [value[k] for k in range(8)]
    sent = short(q3)
    qzy = qzy.at[:, :768].add(wide(swap(sent[:, :768], "x")))
    qzx = qzx.at[:, 768:1408].add(wide(swap(sent[:, 768:1408], "y")))
    qyx = qyx.at[:, 1408:].add(wide(swap(sent[:, 1408:], "zl")))
    qy = qy + wide(swap(short(qyx), "x"))
    qz = qz + wide(swap(short(qzy), "y"))
    qx = qx + wide(swap(short(qzx), "zl"))
    return (
        q0 + wide(swap(short(qx), "x")) + wide(swap(short(qy), "y")) + wide(swap(short(qz), "zl"))
    )


def tensor_parallel(
    resid_in, cotangent, segments, norm_gain, in_proj, conv_weight, conv_bias, x_proj, dt_proj,
    dt_bias, a_log, skip_gain, out_proj,
):
    f32, b16 = jnp.float32, jnp.bfloat16
    model = resid_in.shape[-1]
    zh = lax.axis_index("zh")
    low_half = zh == 0
    own = jnp.stack(
        [
            lax.axis_index("zl"),
            lax.axis_index("y") * 2 + lax.axis_index("x"),
            lax.axis_index("c"),
        ]
    ).astype(jnp.int32)

    def ordered(mine, other):
        return jnp.where(low_half, mine, other), jnp.where(low_half, other, mine)

    out_own = short(out_proj)
    out_other = swap(out_own, "zh")
    rows = jnp.concatenate(
        [
            short(x_proj).T,
            short(dt_proj),
            short(a_log),
            short(conv_weight),
            short(conv_bias)[None],
            short(dt_bias)[None],
            short(skip_gain)[None],
            jnp.zeros((9, 128), b16),
        ],
        axis=0,
    )
    pack = jnp.concatenate(ordered(rows, swap(rows, "zh")), axis=1)
    split = short(in_proj).reshape(64, 2, 2, 16, 128).transpose(3, 1, 0, 2, 4)
    halves = lax.all_to_all(split.reshape(16, 2, 64, 256), GROUP, 0, 0, tiled=True)

    def full_rows(k):
        half = halves[:, k].reshape(1024, 256)
        return jnp.concatenate(ordered(half, swap(half, "zh")), axis=0)

    w_sig, w_gate = full_rows(0), full_rows(1)
    w_out = jnp.concatenate(ordered(out_own, out_other), axis=0)
    gain_own = short(norm_gain)
    gain = lax.all_to_all(
        jnp.broadcast_to(gain_own[None, None], (32, 1, 64)), AXES, 0, 0, tiled=True
    ).reshape(model)
    xp = pack[:160].T
    dt = pack[160:288]
    alog = wide(pack[288:304])
    taps = wide(pack[304:308])
    shift = wide(pack[308:309])
    bias = wide(pack[309:310])
    skip = wide(pack[310:311])
    decay = -jnp.exp(alog)
    rate = jnp.broadcast_to(
        (decay * LOG2E).reshape(16, 1, 2, 128), (16, 4, 2, 128)
    ).reshape(16, 8, 128)

    seg_pair = swap(segments, "zl")
    here = own[0] == 0
    seg = jnp.concatenate(
        [jnp.where(here, segments, seg_pair), jnp.where(here, seg_pair, segments)], axis=0
    )
    padded = jnp.concatenate([jnp.full((4, 3), -1, jnp.int32), seg], axis=1)
    masks = jnp.stack([wide(padded[:, k : k + 512] == seg) for k in range(3)], axis=-1)

    x = wide(resid_in).reshape(128, model)
    blocks = gather_fast(resid_in.reshape(128, model))
    gathered_x = wide(jnp.stack(blocks, axis=0))
    scale_all = lax.rsqrt(jnp.mean(gathered_x * gathered_x, axis=-1, keepdims=True) + EPSILON)
    normed = short(gathered_x * scale_all * wide(gain)).reshape(2048, model)
    rel = (2, 2, 4, 2, 64, 256)
    sig = short(jnp.dot(normed, w_sig, preferred_element_type=f32)).reshape(rel)
    gate = jnp.dot(normed, w_gate, preferred_element_type=f32).reshape(rel)

    absolute = (2, 8, 2, 64)
    act, part = pl.pallas_call(
        conv_kernel,
        grid_spec=pltpu.PrefetchScalarGridSpec(
            num_scalar_prefetch=1,
            grid=(1,),
            in_specs=[whole(rel), whole((4, 512, 3)), whole((4, 256)), whole((1, 256)), whole((256, 160))],
            out_specs=[whole(absolute + (256,)), whole(absolute + (160,))],
            scratch_shapes=[pltpu.VMEM((4, 8, 256), f32), pltpu.VMEM((72, 256), f32)],
        ),
        out_shape=[
            jax.ShapeDtypeStruct(absolute + (256,), b16),
            jax.ShapeDtypeStruct(absolute + (160,), b16),
        ],
        name="conv_forward",
    )(own, sig, masks, taps, shift, xp)

    def summed(parts):
        pieces = lax.all_to_all(parts.reshape(16, 128, 160), GROUP, 0, 0, tiled=True)
        return jnp.sum(wide(pieces), axis=0)

    def to_all(value):
        return lax.all_to_all(
            jnp.broadcast_to(value[None], (16,) + value.shape), GROUP, 0, 0, tiled=True
        )

    total = summed(part)
    high = short(total)
    rest = short(total - wide(high))
    proj = to_all(jnp.concatenate([high, rest[:, 128:]], axis=1)).reshape(absolute + (192,))

    pos = lambda k: (0, k, 0, 0, 0)
    rel_at = lambda k, o: ((k & 1) ^ o[2], 0, (k >> 1) ^ o[1], 0, 0, 0)
    rel_block = (1, 2, 1, 2, 64, 256)
    states, gated, mixer = pl.pallas_call(
        forward_kernel,
        grid_spec=pltpu.PrefetchScalarGridSpec(
            num_scalar_prefetch=1,
            grid=(8,),
            in_specs=[
                pl.BlockSpec((2, 1, 2, 64, 192), lambda k, o: pos(k)),
                pl.BlockSpec((2, 1, 2, 64, 256), lambda k, o: pos(k)),
                pl.BlockSpec(rel_block, rel_at),
                pl.BlockSpec((4, 64, 3), lambda k, o: (0, k, 0)),
                whole((128, 256)),
                whole((1, 256)),
                whole((16, 8, 128)),
                whole((1, 256)),
            ],
            out_specs=[
                pl.BlockSpec((64, 16, 8, 128), lambda k, o: (k, 0, 0, 0)),
                pl.BlockSpec(rel_block, rel_at),
                pl.BlockSpec(rel_block, rel_at),
            ],
            scratch_shapes=[
                pltpu.VMEM((512, 128), f32),
                pltpu.VMEM((512, 128), f32),
                pltpu.VMEM((512, 32), f32),
                pltpu.VMEM((512, 128), f32),
                pltpu.VMEM((16, 8, 128), f32),
            ],
        ),
        out_shape=[
            jax.ShapeDtypeStruct((512, 16, 8, 128), f32),
            jax.ShapeDtypeStruct(rel, b16),
            jax.ShapeDtypeStruct(rel, f32),
        ],
        name="scan_forward",
    )(own, proj, act, gate, masks, dt, bias, rate, skip)

    gated_rows = gated.reshape(2, 1024, 256)
    away = short(jnp.dot(gated_rows[1], w_out, preferred_element_type=f32))
    back = swap(away, "c")
    stay = jnp.dot(gated_rows[0], w_out, preferred_element_type=f32)
    summed_out = scatter_slow(stay.reshape(8, 128, model), back.reshape(8, 128, model))
    resid_out = short(x + summed_out).reshape(2, 64, model)

    upstream = gather_slow(cotangent.reshape(128, model)).reshape(2048, model)
    d_gated = lax.dot_general(
        upstream, w_out, (((1,), (1,)), ((), ())), preferred_element_type=f32
    ).reshape(rel)
    logistic = jax.nn.sigmoid(gate)
    d_mixer = d_gated * (gate * logistic)
    d_gate = short(d_gated * mixer * (logistic * (1.0 + gate * (1.0 - logistic)))).reshape(2048, 256)
    flat = gated.reshape(2048, 2, 128)

    def cols(value, k):
        return lax.dynamic_index_in_dim(value, k, axis=1, keepdims=False)

    def over_tokens(left, right):
        return lax.dot_general(left, right, (((0,), (0,)), ((), ())), preferred_element_type=f32)

    sent = short(over_tokens(cols(flat, 1 - zh), upstream))
    g_out = over_tokens(cols(flat, zh), upstream) + wide(swap(sent, "zh"))

    def halved(grad):
        both = grad.reshape(2, 1024, 256)
        theirs = lax.dynamic_index_in_dim(both, 1 - zh, axis=0, keepdims=False)
        ours = lax.dynamic_index_in_dim(both, zh, axis=0, keepdims=False)
        return short(ours + wide(swap(short(theirs), "zh"))).reshape(16, 64, 256)

    half_gate = halved(over_tokens(normed, d_gate))

    lane_id = jnp.arange(128)[None, :]
    pick = short(wide((jnp.arange(4096) // 128)[:, None] == lane_id))
    rev = lambda k: 7 - k
    dproj_part, d_act, g_rate, g_dt, g_bias, g_skip = pl.pallas_call(
        backward_kernel,
        grid_spec=pltpu.PrefetchScalarGridSpec(
            num_scalar_prefetch=1,
            grid=(8,),
            in_specs=[
                pl.BlockSpec((2, 1, 2, 64, 192), lambda k, o: pos(rev(k))),
                pl.BlockSpec((2, 1, 2, 64, 256), lambda k, o: pos(rev(k))),
                pl.BlockSpec(rel_block, lambda k, o: rel_at(rev(k), o)),
                pl.BlockSpec((4, 64, 3), lambda k, o: (0, rev(k), 0)),
                pl.BlockSpec((64, 16, 8, 128), lambda k, o: (rev(k), 0, 0, 0)),
                pl.BlockSpec(
                    (1, 16, 8, 128), lambda k, o: (jnp.maximum(rev(k) * 64 - 1, 0), 0, 0, 0)
                ),
                whole((128, 256)),
                whole((1, 256)),
                whole((16, 8, 128)),
                whole((1, 256)),
                whole((4096, 128)),
            ],
            out_specs=[
                pl.BlockSpec((2, 1, 2, 64, 160), lambda k, o: pos(rev(k))),
                pl.BlockSpec((2, 1, 2, 64, 256), lambda k, o: pos(rev(k))),
                whole((16, 8, 128)),
                whole((128, 256)),
                whole((1, 256)),
                whole((1, 256)),
            ],
            scratch_shapes=[pltpu.VMEM((512, 128), f32)] * 4
            + [pltpu.VMEM((512, 32), f32)]
            + [pltpu.VMEM((512, 128), f32)] * 2
            + [
                pltpu.VMEM((512, 4096), b16),
                pltpu.VMEM((512, 128), f32),
                pltpu.VMEM((16, 8, 128), f32),
                pltpu.VMEM((256, 128), b16),
                pltpu.VMEM((256, 256), b16),
            ],
        ),
        out_shape=[
            jax.ShapeDtypeStruct(absolute + (160,), b16),
            jax.ShapeDtypeStruct(absolute + (256,), f32),
            jax.ShapeDtypeStruct((16, 8, 128), f32),
            jax.ShapeDtypeStruct((128, 256), f32),
            jax.ShapeDtypeStruct((1, 256), f32),
            jax.ShapeDtypeStruct((1, 256), f32),
        ],
        name="scan_backward",
    )(own, proj, act, d_mixer, masks, states, states, dt, bias, rate, skip, pick)

    dproj = to_all(short(summed(dproj_part))).reshape(absolute + (160,))
    d_sig, g_xp, g_taps, g_shift = pl.pallas_call(
        conv_back_kernel,
        grid_spec=pltpu.PrefetchScalarGridSpec(
            num_scalar_prefetch=1,
            grid=(1,),
            in_specs=[
                whole(rel),
                whole(absolute + (256,)),
                whole(absolute + (256,)),
                whole(absolute + (160,)),
                whole((4, 512, 3)),
                whole((4, 256)),
                whole((1, 256)),
                whole((256, 160)),
            ],
            out_specs=[whole(rel), whole((256, 160)), whole((4, 256)), whole((1, 256))],
            scratch_shapes=[
                pltpu.VMEM((72, 256), f32),
                pltpu.VMEM((4, 3, 8, 256), f32),
                pltpu.VMEM((72, 256), f32),
            ],
        ),
        out_shape=[
            jax.ShapeDtypeStruct(rel, b16),
            jax.ShapeDtypeStruct((256, 160), f32),
            jax.ShapeDtypeStruct((4, 256), f32),
            jax.ShapeDtypeStruct((1, 256), f32),
        ],
        name="conv_backward",
    )(own, sig, act, d_act, dproj, masks, taps, shift, xp)

    d_sig = d_sig.reshape(2, 1024, 256)
    d_gates = d_gate.reshape(2, 1024, 256)

    def into_model(k):
        contract = (((1,), (1,)), ((), ()))
        return lax.dot_general(
            d_sig[k], w_sig, contract, preferred_element_type=f32
        ) + lax.dot_general(d_gates[k], w_gate, contract, preferred_element_type=f32)

    arrived = swap(short(into_model(1)), "c")
    near = (into_model(0) + wide(arrived)).reshape(8, 128, model)
    d_normed = scatter_fast(near)
    half_sig = halved(over_tokens(normed, d_sig.reshape(2048, 256)))
    both = lax.all_to_all(jnp.stack([half_sig, half_gate], axis=1), GROUP, 0, 0, tiled=True)
    g_in = wide(
        both.reshape(16, 2, 64, 2, 128).transpose(2, 1, 3, 0, 4).reshape(64, 8192)
    )
    g_gain = jnp.sum(g_in * wide(short(in_proj)), axis=1) / wide(gain_own)

    scale = lax.rsqrt(jnp.mean(x * x, axis=-1, keepdims=True) + EPSILON)
    weighted = d_normed * wide(gain)
    grad_in = short(
        wide(cotangent).reshape(128, model)
        + scale * weighted
        - x * scale**3 * jnp.mean(x * weighted, axis=-1, keepdims=True)
    ).reshape(2, 64, model)

    g_alog = jnp.sum(g_rate.reshape(16, 4, 2, 128), axis=1).reshape(16, 256) * decay
    grads = jnp.concatenate(
        [g_xp.T, g_dt, g_alog, g_taps, g_shift, g_bias, g_skip, jnp.zeros((9, 256), f32)], axis=0
    ).reshape(320, 2, 128)
    small = cols(grads, zh) + swap(cols(grads, 1 - zh), "zh")
    return (
        resid_out,
        grad_in,
        g_gain,
        g_in,
        small[304:308],
        small[308],
        small[:160].T,
        small[160:288],
        small[309],
        small[288:304],
        small[310],
        g_out,
    )


def solution(mesh):
    in_specs = (
        P("batch", "seq", None),
        P("batch", "seq", None),
        P("batch", None),
        P(("batch", "seq")),
        P(("batch", "seq"), None),
        P(None, ("batch", "seq")),
        P(("batch", "seq")),
        P(("batch", "seq"), None),
        P(None, ("batch", "seq")),
        P(("batch", "seq")),
        P(None, ("batch", "seq")),
        P(("batch", "seq")),
        P(("batch", "seq"), None),
    )
    out_specs = (
        P("batch", "seq", None),
        P("batch", "seq", None),
        P(("batch", "seq")),
        P(("batch", "seq"), None),
        P(None, ("batch", "seq")),
        P(("batch", "seq")),
        P(("batch", "seq"), None),
        P(None, ("batch", "seq")),
        P(("batch", "seq")),
        P(None, ("batch", "seq")),
        P(("batch", "seq")),
        P(("batch", "seq"), None),
    )
    if dict(mesh.shape) != {"batch": 4, "seq": 8}:
        return jax.shard_map(
            on_device, mesh=mesh, in_specs=in_specs, out_specs=out_specs, check_vma=False
        )
    fine = Mesh(mesh.devices.reshape(2, 2, 2, 2, 2), AXES)
    names = {"batch": AXES[:2], "seq": AXES[2:], ("batch", "seq"): AXES}

    def finer(spec):
        return P(*(names.get(entry) for entry in spec))

    return jax.shard_map(
        tensor_parallel,
        mesh=fine,
        in_specs=tuple(finer(s) for s in in_specs),
        out_specs=tuple(finer(s) for s in out_specs),
        check_vma=False,
    )
```
